32 devices in a mesh: ctx: 8 (over y, x, core), exp: 4 (over z).
Axes of the slice: x: 2, y: 2, z: 4, core: 2. Of those that a mesh axis runs over, the one named last changes fastest.
Arguments:
- queries: bfloat16 [4096, 4096], P(('ctx', 'exp')), may hold values from -100 to 100
- keys: bfloat16 [4096, 1024], P(('ctx', 'exp')), may hold values from -100 to 100
- values: bfloat16 [4096, 1024], P(('ctx', 'exp')), may hold values from -6 to 6
- doc_ids: int32 [4096], P(('ctx', 'exp')), may hold values from 0 to 7, never falling along the last dimension, each value on 1 to 1024 neighbouring positions
- span_ids: int32 [4096], P(('ctx', 'exp')), may hold values from 0 to 3, never falling along the last dimension, each value on 1 to 2048 neighbouring positions
Outputs:
- attended: bfloat16 [4096, 4096], P(('ctx', 'exp'))
The draws below stay inside these ranges and needn't reach their ends.
Inputs may be any that keep to these rules, and one draw needn't show every extreme that they name: `doc_ids`: never falling; each document has 1 to 1024 positions, one exactly 1024. `span_ids`: never falling; each span has 1 to 2048 positions, one exactly 2048.
All inputs are finite; a program needn't handle non-finite values.
Results may differ from the reference program's by a relative error of at most 0.0061.
Values may be sent and summed in bfloat16 or wider, within the bound.
A program may use at most 64 MiB of HBM per device.

```python
import math
import jax
import jax.numpy as jnp
import numpy as np
from jax import lax

QUERY_HEADS = 32
KEY_VALUE_HEADS = 8
HEAD_SIZE = 128
SPAN = 8192
DOC_LEN = 2048
PACKED_TOKENS = 4096
SPAN_TOP = 2048
DOC_TOP = 1024
SPANS = 4
DOCS = 8


def broadcast_heads(key, heads):
    key_base, key_rows, key_cols = jax.random.split(key, 3)
    normal_part = jax.random.truncated_normal(key_base, -4.0, 4.0, (PACKED_TOKENS, heads, HEAD_SIZE), jnp.float32)
    row_scale = jnp.exp(jax.random.uniform(key_rows, (PACKED_TOKENS, heads, 1), jnp.float32, 0.0, math.log(10.0)))
    column_scale = jax.random.uniform(key_cols, (1, heads, HEAD_SIZE), jnp.float32, 0.5, 1.5)
    return (normal_part * row_scale * column_scale).reshape(PACKED_TOKENS, heads * HEAD_SIZE)


def draw_queries(key, part):
    return broadcast_heads(jax.random.fold_in(key, 11), QUERY_HEADS).astype(jnp.bfloat16)


def draw_keys(key, part):
    return broadcast_heads(jax.random.fold_in(key, 23), KEY_VALUE_HEADS).astype(jnp.bfloat16)


def steps_of(key, dims, shards, smallest, top_value):
    def one(dim, blocks):
        draws = jax.random.uniform(jax.random.fold_in(jax.random.fold_in(key, 6), dim), (blocks,), jnp.float32, smallest / len(shards), top_value / len(shards))
        return jnp.repeat(jnp.exp(draws), dims[dim] // blocks).reshape((-1,) + (1,) * (len(dims) - dim - 1))

    factor_of = one(*shards[0])
    for cut in shards[1:]:
        factor_of = factor_of * one(*cut)
    return factor_of


def length_profile(number_of, total, reach, skew):
    weights = [(1 << 20) // math.isqrt(grade ** skew) + 1 for grade in range(2, number_of + 1)]
    rest, given = total - reach - (number_of - 1), [1] * (number_of - 1)
    while rest > 0:
        movable = [i for i in range(number_of - 1) if given[i] < reach]
        mass, remaining = sum([weights[i] for i in movable]), rest
        for i in movable:
            more = min(reach - given[i], max(1, remaining * weights[i] // mass), rest)
            given[i] = given[i] + more
            rest = rest - more
    return np.array([reach] + given)


def ragged(own_key, amount, total, limit, lean):
    if amount == 2:
        one = jax.random.randint(own_key, (), max(1, total - limit), min(limit, total - 1) + 1)
        return jnp.stack([one, total - one])
    sizes = jnp.asarray(length_profile(amount, total, limit, lean), jnp.int32)
    twos = (amount - 1) // 2
    donor, sink = sizes[1:1 + 2 * twos:2], sizes[2:2 + 2 * twos:2]
    slack = jnp.minimum(donor - 1, limit - sink)
    moved = jax.random.randint(jax.random.fold_in(own_key, 1), (twos,), 0, 1 << 20) % (slack + 1)
    sizes = sizes.at[1:1 + 2 * twos:2].set(donor - moved).at[2:2 + 2 * twos:2].set(sink + moved)
    return sizes[jax.random.permutation(jax.random.fold_in(own_key, 2), amount)]


def bell_draw(stream_key, shape, spread, limit, shards=(), kind=jnp.bfloat16):
    loudness = steps_of(stream_key, shape, shards, -0.22, 0.18) if shards else 1.0
    drawn = jax.random.normal(stream_key, shape, jnp.float32) * spread * loudness
    return jnp.minimum(jnp.maximum(drawn, -limit), limit).astype(kind)


def setup_inputs(seed: int = 0) -> dict:
    arg_keys = jax.random.split(jax.random.key(seed), 6)
    queries = draw_queries(jax.random.fold_in(arg_keys[5], 71), 0)
    keys = draw_keys(jax.random.fold_in(arg_keys[5], 71), 0)
    values = bell_draw(arg_keys[2], (PACKED_TOKENS, KEY_VALUE_HEADS * HEAD_SIZE), 1.0, 6.0, ((0, 32),))
    doc_ids = jnp.searchsorted(jnp.cumsum(ragged(arg_keys[3], DOCS, PACKED_TOKENS, DOC_TOP, 1)), jnp.arange(PACKED_TOKENS), side="right").astype(jnp.int32)
    span_ids = jnp.searchsorted(jnp.cumsum(ragged(arg_keys[4], SPANS, PACKED_TOKENS, SPAN_TOP, 1)), jnp.arange(PACKED_TOKENS), side="right").astype(jnp.int32)
    return {"queries": queries, "keys": keys, "values": values, "doc_ids": doc_ids, "span_ids": span_ids}


def single_unit_rows(tensor):
    widened = tensor.astype(jnp.float32)
    factor = lax.rsqrt(lax.optimization_barrier(jnp.mean(widened * widened, axis=-1, keepdims=True)) + 1e-06)
    return (widened * factor).astype(jnp.bfloat16)

def reference(queries, keys, values, doc_ids, span_ids):
    overall_rows = queries.shape[0]
    query_heads = single_unit_rows(queries.reshape(overall_rows, QUERY_HEADS, HEAD_SIZE))
    key_head_rows = single_unit_rows(keys.reshape(overall_rows, KEY_VALUE_HEADS, HEAD_SIZE))
    value_head_rows = values.reshape(overall_rows, KEY_VALUE_HEADS, HEAD_SIZE)
    query_group_width = QUERY_HEADS // KEY_VALUE_HEADS
    tile_length = min(512, overall_rows)
    reach_len = min(SPAN, DOC_LEN)
    lookback = (reach_len - 1 + tile_length - 1) // tile_length * tile_length
    window = min(overall_rows, lookback + tile_length)
    offsets_q = jnp.arange(tile_length, dtype=jnp.int32)
    offsets_k = jnp.arange(window, dtype=jnp.int32)

    def one_block(block_num):
        q_first = (block_num * tile_length).astype(jnp.int32)
        k_first = jnp.clip(q_first - lookback, 0, overall_rows - window).astype(jnp.int32)
        query_tile = lax.dynamic_slice_in_dim(query_heads, q_first, tile_length).astype(jnp.float32)
        query_tile = query_tile.reshape(tile_length, KEY_VALUE_HEADS, query_group_width, HEAD_SIZE)
        k_tile = lax.dynamic_slice_in_dim(key_head_rows, k_first, window).astype(jnp.float32)
        v_tile = lax.dynamic_slice_in_dim(value_head_rows, k_first, window).astype(jnp.float32)
        scores = jnp.einsum('qhgd,khd->qhgk', query_tile, k_tile) * HEAD_SIZE ** (-0.5)
        q_pos = q_first + offsets_q
        k_pos = k_first + offsets_k
        q_doc = lax.dynamic_slice_in_dim(doc_ids, q_first, tile_length)
        k_doc = lax.dynamic_slice_in_dim(doc_ids, k_first, window)
        q_span = lax.dynamic_slice_in_dim(span_ids, q_first, tile_length)
        k_span = lax.dynamic_slice_in_dim(span_ids, k_first, window)
        allowed = (q_doc[:, None] == k_doc[None, :]) & (q_span[:, None] == k_span[None, :]) & (k_pos[None, :] <= q_pos[:, None])
        weights = jnp.where(allowed[:, None, None, :], jnp.exp(scores), 0.0)
        totals = lax.optimization_barrier(jnp.sum(weights, axis=3))
        rounded = lax.optimization_barrier(weights.astype(jnp.bfloat16)).astype(jnp.float32)
        numerator = jnp.einsum('qhgk,khd->qhgd', rounded, v_tile)
        return (numerator / totals[..., None]).astype(jnp.bfloat16).reshape(tile_length, QUERY_HEADS * HEAD_SIZE)
    blocks = lax.map(one_block, jnp.arange(overall_rows // tile_length, dtype=jnp.int32))
    return blocks.reshape(overall_rows, QUERY_HEADS * HEAD_SIZE)
```

```python
import math

import jax
import jax.numpy as jnp
from jax import lax
from jax.experimental import pallas as pl
from jax.experimental.pallas import tpu as pltpu
from jax.sharding import PartitionSpec as P

QUERY_HEADS = 32
KEY_VALUE_HEADS = 8
HEAD_SIZE = 128
SPAN = 8192
DOC_LEN = 2048
PACKED_TOKENS = 4096
DOC_TOP = 1024
GROUP = QUERY_HEADS // KEY_VALUE_HEADS
MESH = pl.DeviceIdType.MESH


def shifted(block, axis, distance):
    devices = range(lax.axis_size(axis))
    route = [(i - distance, i) for i in devices if i - distance in devices]
    return lax.ppermute(block, axis, route)


def single_unit_rows(tensor):
    widened = tensor.astype(jnp.float32)
    factor = lax.rsqrt(jnp.mean(widened * widened, axis=-1, keepdims=True) + 1e-06)
    return (widened * factor).astype(jnp.bfloat16)


def general(queries, keys, values, doc_ids, span_ids):
    expanded_size = lax.axis_size("exp")
    ctx_size = lax.axis_size("ctx")
    shard_rows = queries.shape[0]
    shard_len = shard_rows * expanded_size
    query_heads = single_unit_rows(queries.reshape(shard_rows, QUERY_HEADS, HEAD_SIZE))
    key_head_rows = single_unit_rows(keys.reshape(shard_rows, KEY_VALUE_HEADS, HEAD_SIZE))
    value_head_rows = values.reshape(shard_rows, KEY_VALUE_HEADS, HEAD_SIZE)
    head_replicas = max(1, expanded_size // KEY_VALUE_HEADS)
    reach_len = min(SPAN, DOC_LEN)
    steps_back = min((reach_len - 2) // shard_len + 1, ctx_size - 1)
    raw_pair = jnp.concatenate([key_head_rows, value_head_rows], axis=2)

    def spread(pair_rows):
        if head_replicas > 1:
            return jnp.repeat(pair_rows, head_replicas, axis=1)
        return pair_rows

    sources = []
    paired = spread(raw_pair)
    query_local, pair_local = (
        lax.all_to_all(query_heads, "exp", split_axis=1, concat_axis=0, tiled=True),
        lax.all_to_all(paired, "exp", split_axis=1, concat_axis=0, tiled=True),
    )
    block_doc, block_span = (
        lax.all_gather(doc_ids, "exp", axis=0, tiled=True),
        lax.all_gather(span_ids, "exp", axis=0, tiled=True),
    )
    sources.append((0, pair_local, block_doc, block_span))
    for distance in range(1, steps_back + 1):
        moved = shifted(pair_local, "ctx", distance)
        moved_doc, moved_span = shifted((block_doc, block_span), "ctx", distance)
        sources.append((distance, moved, moved_doc, moved_span))
    block_doc = sources[0][2]
    block_span = sources[0][3]
    local_heads = query_local.shape[1]
    pair_heads = sources[0][1].shape[1]
    query_group_width = local_heads // pair_heads
    ctx_index = lax.axis_index("ctx")
    tile_length = min(512, shard_len)
    tiles_side = shard_len // tile_length
    query_start = ctx_index * shard_len
    grouped = query_local.reshape(shard_len, pair_heads, query_group_width, HEAD_SIZE)
    inv_root = HEAD_SIZE ** (-0.5)
    offsets = jnp.arange(tile_length, dtype=jnp.int32)
    query_doc_tiles = block_doc.reshape(tiles_side, tile_length)
    query_span_tiles = block_span.reshape(tiles_side, tile_length)
    numer_list = [
        jnp.zeros((tile_length, pair_heads, query_group_width, HEAD_SIZE), jnp.float32)
        for _ in range(tiles_side)
    ]
    denom_list = [
        jnp.zeros((tile_length, pair_heads, query_group_width), jnp.float32)
        for _ in range(tiles_side)
    ]
    for distance, source, key_doc, key_span in sources:
        key_start = query_start - distance * shard_len
        present = ctx_index >= distance
        key_doc_tiles = key_doc.reshape(tiles_side, tile_length)
        key_span_tiles = key_span.reshape(tiles_side, tile_length)
        live_table = (
            (key_doc_tiles[None, :, tile_length - 1] >= query_doc_tiles[:, None, 0])
            & (key_span_tiles[None, :, tile_length - 1] >= query_span_tiles[:, None, 0])
            & present
        )
        for q_block in range(tiles_side):
            for k_block in range(tiles_side):
                q_first = q_block * tile_length
                k_first = k_block * tile_length
                static_gap = distance * shard_len + q_first - k_first
                if static_gap + tile_length - 1 < 0:
                    continue
                if static_gap - (tile_length - 1) > reach_len - 1:
                    continue

                def compute(
                    inner_acc,
                    source=source,
                    key_start=key_start,
                    q_first=q_first,
                    k_first=k_first,
                    key_doc_tiles=key_doc_tiles,
                    key_span_tiles=key_span_tiles,
                    q_block=q_block,
                    k_block=k_block,
                ):
                    numer_in, denom_in = inner_acc
                    query_tile = grouped[q_first : q_first + tile_length]
                    kv_tile = source[k_first : k_first + tile_length]
                    scores = (
                        jnp.einsum(
                            "qhgd,khd->qhgk",
                            query_tile,
                            kv_tile[:, :, :HEAD_SIZE],
                            preferred_element_type=jnp.float32,
                        )
                        * inv_root
                    )
                    q_pos = query_start + q_first + offsets
                    k_pos = key_start + k_first + offsets
                    q_doc_t = query_doc_tiles[q_block]
                    q_span_t = query_span_tiles[q_block]
                    k_doc_t = key_doc_tiles[k_block]
                    k_span_t = key_span_tiles[k_block]
                    allowed = (
                        (q_doc_t[:, None] == k_doc_t[None, :])
                        & (q_span_t[:, None] == k_span_t[None, :])
                        & (k_pos[None, :] <= q_pos[:, None])
                    )
                    weights = jnp.where(allowed[:, None, None, :], jnp.exp(scores), 0.0)
                    part_den = jnp.sum(weights, axis=3)
                    part_num = jnp.einsum(
                        "qhgk,khd->qhgd",
                        weights.astype(jnp.bfloat16),
                        kv_tile[:, :, HEAD_SIZE:],
                        preferred_element_type=jnp.float32,
                    )
                    return (numer_in + part_num, denom_in + part_den)

                numer_list[q_block], denom_list[q_block] = lax.cond(
                    live_table[q_block, k_block],
                    compute,
                    lambda inner_acc: inner_acc,
                    (numer_list[q_block], denom_list[q_block]),
                )
    numerator = jnp.concatenate(numer_list, axis=0)
    denominator = jnp.concatenate(denom_list, axis=0)
    attended = (
        (numerator / denominator[..., None])
        .astype(jnp.bfloat16)
        .reshape(shard_len, local_heads, HEAD_SIZE)
    )
    returned = lax.all_to_all(attended, "exp", split_axis=0, concat_axis=1, tiled=True)
    return returned.reshape(shard_rows, QUERY_HEADS * HEAD_SIZE)


def unit_tile(tile):
    widened = tile.astype(jnp.float32)
    factor = lax.rsqrt(jnp.mean(widened * widened, axis=-1, keepdims=True) + 1e-06)
    return (widened * factor).astype(jnp.bfloat16)


def relay_kernel(
    blocks, lanes, q_ref, k_ref, v_ref, id_ref, out_ref,
    q_raw, q_unit, k_all, v_all, id_all, own_col, acc,
    own_sem, recv_sem, send_sem,
):
    rows = k_ref.shape[0]
    ctx = lax.axis_index("ctx")
    z = lax.axis_index("exp")
    even = ctx % 2 == 0
    inputs = (k_ref, v_ref, id_ref)
    slots = (k_all, v_all, id_all)

    barrier = pltpu.get_barrier_semaphore()
    neighbours = [
        (z > 0, (ctx, z - 1)), (z < lanes - 1, (ctx, z + 1)),
        (ctx > 0, (ctx - 1, z)), (ctx < blocks - 1, (ctx + 1, z)),
        (ctx > 1, (ctx - 2, z)), (ctx < blocks - 2, (ctx + 2, z)),
    ]
    for present, device in neighbours:
        @pl.when(present)
        def _(device=device):
            pl.semaphore_signal(barrier, inc=1, device_id=device, device_id_type=MESH)
    pl.semaphore_wait(barrier, sum(present.astype(jnp.int32) for present, _ in neighbours))

    def send(way, b, zp, device, to_b, own, finish):
        for part in range(3):
            source = inputs[part] if own else slots[part].at[b * lanes + zp]
            copy = pltpu.make_async_remote_copy(
                src_ref=source,
                dst_ref=slots[part].at[to_b * lanes + zp],
                send_sem=send_sem.at[way, b * lanes + zp, part],
                recv_sem=recv_sem.at[to_b * lanes + zp, part],
                device_id=device,
                device_id_type=MESH,
            )
            if finish:
                copy.wait_send()
            else:
                copy.start()

    def forward(b, zp, own=False, finish=False):
        routes = []
        if b == 0:
            routes.append((0, (zp <= z) & (z < lanes - 1), (ctx, z + 1), 0))
        if b <= 1:
            routes.append((1, even & (z > 0) & (zp >= z), (ctx, z - 1), b))
        if b == 0:
            routes.append((2, even | ((zp <= z) & (ctx < blocks - 1)), (ctx + 1, z), 1))
            routes.append((3, even & (zp >= z) & (ctx < blocks - 2), (ctx + 2, z), 2))
        if b == 1:
            routes.append((2, even & (zp >= z), (ctx + 1, z), 2))
        for way, taken, device, to_b in routes:
            @pl.when(taken)
            def _(way=way, device=device, to_b=to_b):
                send(way, b, zp, device, to_b, own, finish)

    forward(0, z, own=True)

    own_copies = [
        pltpu.make_async_copy(inputs[part], slots[part].at[z], own_sem.at[part]) for part in range(3)
    ]
    q_copy = pltpu.make_async_copy(q_ref, q_raw, own_sem.at[3])
    for copy in [q_copy] + own_copies:
        copy.start()
    acc[...] = jnp.zeros_like(acc)
    q_copy.wait()

    @pl.loop(0, KEY_VALUE_HEADS)
    def _(g):
        for j in range(GROUP):
            column = pl.multiple_of((g * GROUP + j) * HEAD_SIZE, HEAD_SIZE)
            q_unit[g, pl.ds(j * rows, rows), :] = unit_tile(q_raw[:, pl.ds(column, HEAD_SIZE)])

    for copy in own_copies:
        copy.wait()
    own_row = id_all[z][0:1, :]
    own_col[...] = jnp.broadcast_to(own_row, (rows, rows)).T

    scale = math.log2(math.e) * HEAD_SIZE ** (-0.5)

    def attend(slot, own=False):
        same = own_col[...] == jnp.broadcast_to(id_all[slot][0:1, :], (rows, rows))
        if own:
            same = same & (
                lax.broadcasted_iota(jnp.int32, (rows, rows), 1)
                <= lax.broadcasted_iota(jnp.int32, (rows, rows), 0)
            )
        same = jnp.concatenate([same.astype(jnp.float32)] * GROUP, axis=0) > 0.5
        ones = jnp.ones((rows, HEAD_SIZE), jnp.bfloat16)

        @pl.loop(0, KEY_VALUE_HEADS)
        def _(g):
            column = pl.ds(pl.multiple_of(g * HEAD_SIZE, HEAD_SIZE), HEAD_SIZE)
            key = unit_tile(k_all[slot, :, column])
            scores = lax.dot_general(
                q_unit[g], key, (((1,), (1,)), ((), ())), preferred_element_type=jnp.float32
            )
            weights = jnp.where(same, jnp.exp2(scores * scale), 0.0).astype(jnp.bfloat16)
            value = jnp.concatenate([v_all[slot, :, column], ones], axis=1)
            acc[g] += jnp.dot(weights, value, preferred_element_type=jnp.float32)

    attend(z, own=True)

    def receive(b, zp, needed):
        slot = b * lanes + zp
        for part in range(3):
            pltpu.make_async_remote_copy(
                src_ref=slots[part].at[slot],
                dst_ref=slots[part].at[slot],
                send_sem=send_sem.at[0, slot, part],
                recv_sem=recv_sem.at[slot, part],
                device_id=(ctx, z),
                device_id_type=MESH,
            ).wait_recv()
        forward(b, zp)
        if needed:
            attend(slot)

    @pl.loop(0, lanes)
    def _(d):
        for b, zp, valid, needed in (
            (0, z - d - 1, z - d - 1 >= 0, True),
            (0, z + d + 1, even & (z + d + 1 < lanes), False),
            (1, z + d, (ctx > 0) & (z + d < lanes), True),
            (1, z - d, (ctx > 0) & (z - d >= 0) & (d > 0), True),
            (2, z + d, (ctx > 1) & (z + d < lanes), True),
        ):
            @pl.when(valid)
            def _(b=b, zp=zp, needed=needed):
                receive(b, zp, needed)

    @pl.loop(0, KEY_VALUE_HEADS)
    def _(g):
        for j in range(GROUP):
            column = pl.multiple_of((g * GROUP + j) * HEAD_SIZE, HEAD_SIZE)
            part = acc[g, pl.ds(j * rows, rows), :]
            out_ref[:, pl.ds(column, HEAD_SIZE)] = (
                part[:, :HEAD_SIZE] / part[:, HEAD_SIZE:]
            ).astype(jnp.bfloat16)

    @pl.loop(0, lanes)
    def _(zp):
        @pl.when((zp <= z) | even)
        def _():
            forward(0, zp, finish=True)

        @pl.when(ctx > 0)
        def _():
            forward(1, zp, finish=True)


def relayed(queries, keys, values, doc_ids, span_ids):
    lanes = lax.axis_size("exp")
    blocks = lax.axis_size("ctx")
    rows = queries.shape[0]
    codes = jnp.broadcast_to((doc_ids * 65536 + span_ids)[None, :], (8, rows))
    count = 3 * lanes
    bf16, f32 = jnp.bfloat16, jnp.float32
    return pl.pallas_call(
        lambda *refs: relay_kernel(blocks, lanes, *refs),
        out_shape=jax.ShapeDtypeStruct(queries.shape, bf16),
        in_specs=[pl.BlockSpec(memory_space=pl.ANY)] * 4,
        out_specs=pl.BlockSpec(memory_space=pltpu.VMEM),
        scratch_shapes=[
            pltpu.VMEM(queries.shape, bf16),
            pltpu.VMEM((KEY_VALUE_HEADS, GROUP * rows, HEAD_SIZE), bf16),
            pltpu.VMEM((count,) + keys.shape, bf16),
            pltpu.VMEM((count,) + values.shape, bf16),
            pltpu.VMEM((count, 8, rows), jnp.int32),
            pltpu.VMEM((rows, rows), jnp.int32),
            pltpu.VMEM((KEY_VALUE_HEADS, GROUP * rows, 2 * HEAD_SIZE), f32),
            pltpu.SemaphoreType.DMA((4,)),
            pltpu.SemaphoreType.DMA((count, 3)),
            pltpu.SemaphoreType.DMA((4, count, 3)),
        ],
        compiler_params=pltpu.CompilerParams(collective_id=0, has_side_effects=True),
    )(queries, keys, values, codes)


def per_device(queries, keys, values, doc_ids, span_ids):
    lanes, blocks = lax.axis_size("exp"), lax.axis_size("ctx")
    rows = queries.shape[0]
    tokens = rows * lanes * blocks
    reach = min(SPAN, DOC_LEN if tokens > PACKED_TOKENS else DOC_TOP)
    if reach <= 2 * lanes * rows and blocks % 2 == 0 and lanes <= 8 and rows % 128 == 0:
        return relayed(queries, keys, values, doc_ids, span_ids)
    return general(queries, keys, values, doc_ids, span_ids)


def solution(mesh):
    in_specs = (
        P(("ctx", "exp"), None),
        P(("ctx", "exp"), None),
        P(("ctx", "exp"), None),
        P(("ctx", "exp")),
        P(("ctx", "exp")),
    )
    out_specs = P(("ctx", "exp"), None)
    return jax.shard_map(
        per_device, mesh=mesh, in_specs=in_specs, out_specs=out_specs, check_vma=False
    )
```

```python
import math

import jax
import jax.numpy as jnp
from jax import lax
from jax.experimental import pallas as pl
from jax.experimental.pallas import tpu as pltpu
from jax.sharding import PartitionSpec as P

QUERY_HEADS = 32
KEY_VALUE_HEADS = 8
HEAD_SIZE = 128
SPAN = 8192
DOC_LEN = 2048
PACKED_TOKENS = 4096
DOC_TOP = 1024
GROUP = QUERY_HEADS // KEY_VALUE_HEADS
MESH = pl.DeviceIdType.MESH


def shifted(block, axis, distance):
    devices = range(lax.axis_size(axis))
    route = [(i - distance, i) for i in devices if i - distance in devices]
    return lax.ppermute(block, axis, route)


def single_unit_rows(tensor):
    widened = tensor.astype(jnp.float32)
    factor = lax.rsqrt(jnp.mean(widened * widened, axis=-1, keepdims=True) + 1e-06)
    return (widened * factor).astype(jnp.bfloat16)


def general(queries, keys, values, doc_ids, span_ids):
    expanded_size = lax.axis_size("exp")
    ctx_size = lax.axis_size("ctx")
    shard_rows = queries.shape[0]
    shard_len = shard_rows * expanded_size
    query_heads = single_unit_rows(queries.reshape(shard_rows, QUERY_HEADS, HEAD_SIZE))
    key_head_rows = single_unit_rows(keys.reshape(shard_rows, KEY_VALUE_HEADS, HEAD_SIZE))
    value_head_rows = values.reshape(shard_rows, KEY_VALUE_HEADS, HEAD_SIZE)
    head_replicas = max(1, expanded_size // KEY_VALUE_HEADS)
    reach_len = min(SPAN, DOC_LEN)
    steps_back = min((reach_len - 2) // shard_len + 1, ctx_size - 1)
    raw_pair = jnp.concatenate([key_head_rows, value_head_rows], axis=2)

    def spread(pair_rows):
        if head_replicas > 1:
            return jnp.repeat(pair_rows, head_replicas, axis=1)
        return pair_rows

    sources = []
    paired = spread(raw_pair)
    query_local, pair_local = (
        lax.all_to_all(query_heads, "exp", split_axis=1, concat_axis=0, tiled=True),
        lax.all_to_all(paired, "exp", split_axis=1, concat_axis=0, tiled=True),
    )
    block_doc, block_span = (
        lax.all_gather(doc_ids, "exp", axis=0, tiled=True),
        lax.all_gather(span_ids, "exp", axis=0, tiled=True),
    )
    sources.append((0, pair_local, block_doc, block_span))
    for distance in range(1, steps_back + 1):
        moved = shifted(pair_local, "ctx", distance)
        moved_doc, moved_span = shifted((block_doc, block_span), "ctx", distance)
        sources.append((distance, moved, moved_doc, moved_span))
    block_doc = sources[0][2]
    block_span = sources[0][3]
    local_heads = query_local.shape[1]
    pair_heads = sources[0][1].shape[1]
    query_group_width = local_heads // pair_heads
    ctx_index = lax.axis_index("ctx")
    tile_length = min(512, shard_len)
    tiles_side = shard_len // tile_length
    query_start = ctx_index * shard_len
    grouped = query_local.reshape(shard_len, pair_heads, query_group_width, HEAD_SIZE)
    inv_root = HEAD_SIZE ** (-0.5)
    offsets = jnp.arange(tile_length, dtype=jnp.int32)
    query_doc_tiles = block_doc.reshape(tiles_side, tile_length)
    query_span_tiles = block_span.reshape(tiles_side, tile_length)
    numer_list = [
        jnp.zeros((tile_length, pair_heads, query_group_width, HEAD_SIZE), jnp.float32)
        for _ in range(tiles_side)
    ]
    denom_list = [
        jnp.zeros((tile_length, pair_heads, query_group_width), jnp.float32)
        for _ in range(tiles_side)
    ]
    for distance, source, key_doc, key_span in sources:
        key_start = query_start - distance * shard_len
        present = ctx_index >= distance
        key_doc_tiles = key_doc.reshape(tiles_side, tile_length)
        key_span_tiles = key_span.reshape(tiles_side, tile_length)
        live_table = (
            (key_doc_tiles[None, :, tile_length - 1] >= query_doc_tiles[:, None, 0])
            & (key_span_tiles[None, :, tile_length - 1] >= query_span_tiles[:, None, 0])
            & present
        )
        for q_block in range(tiles_side):
            for k_block in range(tiles_side):
                q_first = q_block * tile_length
                k_first = k_block * tile_length
                static_gap = distance * shard_len + q_first - k_first
                if static_gap + tile_length - 1 < 0:
                    continue
                if static_gap - (tile_length - 1) > reach_len - 1:
                    continue

                def compute(
                    inner_acc,
                    source=source,
                    key_start=key_start,
                    q_first=q_first,
                    k_first=k_first,
                    key_doc_tiles=key_doc_tiles,
                    key_span_tiles=key_span_tiles,
                    q_block=q_block,
                    k_block=k_block,
                ):
                    numer_in, denom_in = inner_acc
                    query_tile = grouped[q_first : q_first + tile_length]
                    kv_tile = source[k_first : k_first + tile_length]
                    scores = (
                        jnp.einsum(
                            "qhgd,khd->qhgk",
                            query_tile,
                            kv_tile[:, :, :HEAD_SIZE],
                            preferred_element_type=jnp.float32,
                        )
                        * inv_root
                    )
                    q_pos = query_start + q_first + offsets
                    k_pos = key_start + k_first + offsets
                    q_doc_t = query_doc_tiles[q_block]
                    q_span_t = query_span_tiles[q_block]
                    k_doc_t = key_doc_tiles[k_block]
                    k_span_t = key_span_tiles[k_block]
                    allowed = (
                        (q_doc_t[:, None] == k_doc_t[None, :])
                        & (q_span_t[:, None] == k_span_t[None, :])
                        & (k_pos[None, :] <= q_pos[:, None])
                    )
                    weights = jnp.where(allowed[:, None, None, :], jnp.exp(scores), 0.0)
                    part_den = jnp.sum(weights, axis=3)
                    part_num = jnp.einsum(
                        "qhgk,khd->qhgd",
                        weights.astype(jnp.bfloat16),
                        kv_tile[:, :, HEAD_SIZE:],
                        preferred_element_type=jnp.float32,
                    )
                    return (numer_in + part_num, denom_in + part_den)

                numer_list[q_block], denom_list[q_block] = lax.cond(
                    live_table[q_block, k_block],
                    compute,
                    lambda inner_acc: inner_acc,
                    (numer_list[q_block], denom_list[q_block]),
                )
    numerator = jnp.concatenate(numer_list, axis=0)
    denominator = jnp.concatenate(denom_list, axis=0)
    attended = (
        (numerator / denominator[..., None])
        .astype(jnp.bfloat16)
        .reshape(shard_len, local_heads, HEAD_SIZE)
    )
    returned = lax.all_to_all(attended, "exp", split_axis=0, concat_axis=1, tiled=True)
    return returned.reshape(shard_rows, QUERY_HEADS * HEAD_SIZE)


def unit_tile(tile):
    widened = tile.astype(jnp.float32)
    factor = lax.rsqrt(jnp.mean(widened * widened, axis=-1, keepdims=True) + 1e-06)
    return (widened * factor).astype(jnp.bfloat16)


def relay_kernel(
    blocks, lanes, q_ref, k_ref, v_ref, doc_ref, span_ref, out_ref,
    q_raw, q_unit, k_all, v_all, id_all, own_col, acc,
    own_sem, recv_sem, send_sem,
):
    rows = k_ref.shape[0]
    ctx = lax.axis_index("ctx")
    z = lax.axis_index("exp")
    even = ctx % 2 == 0
    slots = (k_all, v_all, id_all)
    inputs = (k_ref, v_ref, id_all.at[z])

    barrier = pltpu.get_barrier_semaphore()
    neighbours = [
        (z > 0, (ctx, z - 1)), (z < lanes - 1, (ctx, z + 1)),
        (ctx > 0, (ctx - 1, z)), (ctx < blocks - 1, (ctx + 1, z)),
        (ctx > 1, (ctx - 2, z)), (ctx < blocks - 2, (ctx + 2, z)),
    ]
    for present, device in neighbours:
        @pl.when(present)
        def _(device=device):
            pl.semaphore_signal(barrier, inc=1, device_id=device, device_id_type=MESH)
    pl.semaphore_wait(barrier, sum(present.astype(jnp.int32) for present, _ in neighbours))

    def send(way, b, zp, device, to_b, part, own, finish):
        copy = pltpu.make_async_remote_copy(
            src_ref=inputs[part] if own else slots[part].at[b * lanes + zp],
            dst_ref=slots[part].at[to_b * lanes + zp],
            send_sem=send_sem.at[way, b * lanes + zp, part],
            recv_sem=recv_sem.at[to_b * lanes + zp, part],
            device_id=device,
            device_id_type=MESH,
        )
        if finish:
            copy.wait_send()
        else:
            copy.start()

    def forward(b, zp, parts=(0, 1, 2), ways=(0, 1, 2, 3), own=False, finish=False):
        routes = []
        if b <= 1:
            routes.append((1, even & (z > 0) & (zp >= z), (ctx, z - 1), b))
        if b == 0:
            routes.append((2, even | ((zp <= z) & (ctx < blocks - 1)), (ctx + 1, z), 1))
            routes.append((0, (zp <= z) & (z < lanes - 1), (ctx, z + 1), 0))
            routes.append((3, even & (zp >= z) & (ctx < blocks - 2), (ctx + 2, z), 2))
        if b == 1:
            routes.append((2, even & (zp >= z), (ctx + 1, z), 2))
        for way, taken, device, to_b in routes:
            if way in ways:
                @pl.when(taken)
                def _(way=way, device=device, to_b=to_b):
                    for part in parts:
                        send(way, b, zp, device, to_b, part, own, finish)

    forward(0, z, parts=(0, 1), ways=(0, 1, 2), own=True)

    id_copies = [
        pltpu.make_async_copy(ref, id_all.at[z, pl.ds(row, 1)], own_sem.at[row])
        for row, ref in enumerate((doc_ref, span_ref))
    ]
    own_copies = [
        pltpu.make_async_copy(inputs[part], slots[part].at[z], own_sem.at[2 + part]) for part in range(2)
    ]
    q_copy = pltpu.make_async_copy(q_ref, q_raw, own_sem.at[4])
    for copy in id_copies + [q_copy] + own_copies:
        copy.start()
    for copy in id_copies:
        copy.wait()
    forward(0, z, parts=(2,), ways=(0, 1, 2), own=True)
    acc[...] = jnp.zeros_like(acc)
    q_copy.wait()

    @pl.loop(0, KEY_VALUE_HEADS, unroll=4)
    def _(g):
        for j in range(GROUP):
            column = pl.multiple_of((g * GROUP + j) * HEAD_SIZE, HEAD_SIZE)
            q_unit[g, pl.ds(j * rows, rows), :] = unit_tile(q_raw[:, pl.ds(column, HEAD_SIZE)])

    for copy in own_copies:
        copy.wait()

    def codes(slot):
        ids = id_all[slot]
        return jnp.broadcast_to(ids[0:1, :] * 65536 + ids[1:2, :], (rows, rows))

    own_col[...] = codes(z).T

    scale = math.log2(math.e) * HEAD_SIZE ** (-0.5)

    def attend(slot, own=False):
        same = own_col[...] == codes(slot)
        if own:
            same = same & (
                lax.broadcasted_iota(jnp.int32, (rows, rows), 1)
                <= lax.broadcasted_iota(jnp.int32, (rows, rows), 0)
            )
        kept = same.astype(jnp.float32).astype(jnp.bfloat16)
        ones = jnp.ones((rows, HEAD_SIZE), jnp.bfloat16)

        @pl.loop(0, KEY_VALUE_HEADS, unroll=KEY_VALUE_HEADS)
        def _(g):
            column = pl.ds(pl.multiple_of(g * HEAD_SIZE, HEAD_SIZE), HEAD_SIZE)
            key = unit_tile(k_all[slot, :, column])
            scores = lax.dot_general(
                q_unit[g], key, (((1,), (1,)), ((), ())), preferred_element_type=jnp.float32
            )
            weights = jnp.exp2(scores * scale).astype(jnp.bfloat16)
            weights = jnp.concatenate(
                [weights[j * rows : (j + 1) * rows] * kept for j in range(GROUP)], axis=0
            )
            value = jnp.concatenate([v_all[slot, :, column], ones], axis=1)
            acc[g] += jnp.dot(weights, value, preferred_element_type=jnp.float32)

    attend(z, own=True)
    forward(0, z, ways=(3,), own=True)

    def receive(b, zp, needed):
        slot = b * lanes + zp
        for part in range(3):
            pltpu.make_async_remote_copy(
                src_ref=slots[part].at[slot],
                dst_ref=slots[part].at[slot],
                send_sem=send_sem.at[0, slot, part],
                recv_sem=recv_sem.at[slot, part],
                device_id=(ctx, z),
                device_id_type=MESH,
            ).wait_recv()
            forward(b, zp, parts=(part,))
        if needed:
            attend(slot)

    @pl.loop(0, lanes)
    def _(d):
        for b, zp, valid, needed in (
            (0, z + d + 1, even & (z + d + 1 < lanes), False),
            (1, z + d, (ctx > 0) & (z + d < lanes), True),
            (0, z - d - 1, z - d - 1 >= 0, True),
            (1, z - d, (ctx > 0) & (z - d >= 0) & (d > 0), True),
            (2, z + d, (ctx > 1) & (z + d < lanes), True),
        ):
            @pl.when(valid)
            def _(b=b, zp=zp, needed=needed):
                receive(b, zp, needed)

    @pl.loop(0, KEY_VALUE_HEADS, unroll=4)
    def _(g):
        for j in range(GROUP):
            column = pl.multiple_of((g * GROUP + j) * HEAD_SIZE, HEAD_SIZE)
            part = acc[g, pl.ds(j * rows, rows), :]
            out_ref[:, pl.ds(column, HEAD_SIZE)] = (
                part[:, :HEAD_SIZE] / part[:, HEAD_SIZE:]
            ).astype(jnp.bfloat16)

    @pl.loop(0, lanes)
    def _(zp):
        @pl.when((zp <= z) | even)
        def _():
            forward(0, zp, finish=True)

        @pl.when(ctx > 0)
        def _():
            forward(1, zp, finish=True)


def relayed(queries, keys, values, doc_ids, span_ids):
    lanes = lax.axis_size("exp")
    blocks = lax.axis_size("ctx")
    rows = queries.shape[0]
    count = 3 * lanes
    bf16, f32 = jnp.bfloat16, jnp.float32
    return pl.pallas_call(
        lambda *refs: relay_kernel(blocks, lanes, *refs),
        out_shape=jax.ShapeDtypeStruct(queries.shape, bf16),
        in_specs=[pl.BlockSpec(memory_space=pl.ANY)] * 5,
        out_specs=pl.BlockSpec(memory_space=pltpu.VMEM),
        scratch_shapes=[
            pltpu.VMEM(queries.shape, bf16),
            pltpu.VMEM((KEY_VALUE_HEADS, GROUP * rows, HEAD_SIZE), bf16),
            pltpu.VMEM((count,) + keys.shape, bf16),
            pltpu.VMEM((count,) + values.shape, bf16),
            pltpu.VMEM((count, 2, rows), jnp.int32),
            pltpu.VMEM((rows, rows), jnp.int32),
            pltpu.VMEM((KEY_VALUE_HEADS, GROUP * rows, 2 * HEAD_SIZE), f32),
            pltpu.SemaphoreType.DMA((5,)),
            pltpu.SemaphoreType.DMA((count, 3)),
            pltpu.SemaphoreType.DMA((4, count, 3)),
        ],
        compiler_params=pltpu.CompilerParams(collective_id=0, has_side_effects=True),
    )(queries, keys, values, doc_ids[None, :], span_ids[None, :])


def per_device(queries, keys, values, doc_ids, span_ids):
    lanes, blocks = lax.axis_size("exp"), lax.axis_size("ctx")
    rows = queries.shape[0]
    tokens = rows * lanes * blocks
    reach = min(SPAN, DOC_LEN if tokens > PACKED_TOKENS else DOC_TOP)
    if reach <= 2 * lanes * rows and blocks % 2 == 0 and lanes <= 8 and rows % 128 == 0:
        return relayed(queries, keys, values, doc_ids, span_ids)
    return general(queries, keys, values, doc_ids, span_ids)


def solution(mesh):
    in_specs = (
        P(("ctx", "exp"), None),
        P(("ctx", "exp"), None),
        P(("ctx", "exp"), None),
        P(("ctx", "exp")),
        P(("ctx", "exp")),
    )
    out_specs = P(("ctx", "exp"), None)
    return jax.shard_map(
        per_device, mesh=mesh, in_specs=in_specs, out_specs=out_specs, check_vma=False
    )
```

```python
import math

import jax
import jax.numpy as jnp
from jax import lax
from jax.experimental import pallas as pl
from jax.experimental.pallas import tpu as pltpu
from jax.sharding import PartitionSpec as P

QUERY_HEADS = 32
KEY_VALUE_HEADS = 8
HEAD_SIZE = 128
SPAN = 8192
DOC_LEN = 2048
PACKED_TOKENS = 4096
DOC_TOP = 1024
GROUP = QUERY_HEADS // KEY_VALUE_HEADS
MESH = pl.DeviceIdType.MESH


def shifted(block, axis, distance):
    devices = range(lax.axis_size(axis))
    route = [(i - distance, i) for i in devices if i - distance in devices]
    return lax.ppermute(block, axis, route)


def single_unit_rows(tensor):
    widened = tensor.astype(jnp.float32)
    factor = lax.rsqrt(jnp.mean(widened * widened, axis=-1, keepdims=True) + 1e-06)
    return (widened * factor).astype(jnp.bfloat16)


def general(queries, keys, values, doc_ids, span_ids):
    expanded_size = lax.axis_size("exp")
    ctx_size = lax.axis_size("ctx")
    shard_rows = queries.shape[0]
    shard_len = shard_rows * expanded_size
    query_heads = single_unit_rows(queries.reshape(shard_rows, QUERY_HEADS, HEAD_SIZE))
    key_head_rows = single_unit_rows(keys.reshape(shard_rows, KEY_VALUE_HEADS, HEAD_SIZE))
    value_head_rows = values.reshape(shard_rows, KEY_VALUE_HEADS, HEAD_SIZE)
    head_replicas = max(1, expanded_size // KEY_VALUE_HEADS)
    reach_len = min(SPAN, DOC_LEN)
    steps_back = min((reach_len - 2) // shard_len + 1, ctx_size - 1)
    raw_pair = jnp.concatenate([key_head_rows, value_head_rows], axis=2)

    def spread(pair_rows):
        if head_replicas > 1:
            return jnp.repeat(pair_rows, head_replicas, axis=1)
        return pair_rows

    sources = []
    paired = spread(raw_pair)
    query_local, pair_local = (
        lax.all_to_all(query_heads, "exp", split_axis=1, concat_axis=0, tiled=True),
        lax.all_to_all(paired, "exp", split_axis=1, concat_axis=0, tiled=True),
    )
    block_doc, block_span = (
        lax.all_gather(doc_ids, "exp", axis=0, tiled=True),
        lax.all_gather(span_ids, "exp", axis=0, tiled=True),
    )
    sources.append((0, pair_local, block_doc, block_span))
    for distance in range(1, steps_back + 1):
        moved = shifted(pair_local, "ctx", distance)
        moved_doc, moved_span = shifted((block_doc, block_span), "ctx", distance)
        sources.append((distance, moved, moved_doc, moved_span))
    block_doc = sources[0][2]
    block_span = sources[0][3]
    local_heads = query_local.shape[1]
    pair_heads = sources[0][1].shape[1]
    query_group_width = local_heads // pair_heads
    ctx_index = lax.axis_index("ctx")
    tile_length = min(512, shard_len)
    tiles_side = shard_len // tile_length
    query_start = ctx_index * shard_len
    grouped = query_local.reshape(shard_len, pair_heads, query_group_width, HEAD_SIZE)
    inv_root = HEAD_SIZE ** (-0.5)
    offsets = jnp.arange(tile_length, dtype=jnp.int32)
    query_doc_tiles = block_doc.reshape(tiles_side, tile_length)
    query_span_tiles = block_span.reshape(tiles_side, tile_length)
    numer_list = [
        jnp.zeros((tile_length, pair_heads, query_group_width, HEAD_SIZE), jnp.float32)
        for _ in range(tiles_side)
    ]
    denom_list = [
        jnp.zeros((tile_length, pair_heads, query_group_width), jnp.float32)
        for _ in range(tiles_side)
    ]
    for distance, source, key_doc, key_span in sources:
        key_start = query_start - distance * shard_len
        present = ctx_index >= distance
        key_doc_tiles = key_doc.reshape(tiles_side, tile_length)
        key_span_tiles = key_span.reshape(tiles_side, tile_length)
        live_table = (
            (key_doc_tiles[None, :, tile_length - 1] >= query_doc_tiles[:, None, 0])
            & (key_span_tiles[None, :, tile_length - 1] >= query_span_tiles[:, None, 0])
            & present
        )
        for q_block in range(tiles_side):
            for k_block in range(tiles_side):
                q_first = q_block * tile_length
                k_first = k_block * tile_length
                static_gap = distance * shard_len + q_first - k_first
                if static_gap + tile_length - 1 < 0:
                    continue
                if static_gap - (tile_length - 1) > reach_len - 1:
                    continue

                def compute(
                    inner_acc,
                    source=source,
                    key_start=key_start,
                    q_first=q_first,
                    k_first=k_first,
                    key_doc_tiles=key_doc_tiles,
                    key_span_tiles=key_span_tiles,
                    q_block=q_block,
                    k_block=k_block,
                ):
                    numer_in, denom_in = inner_acc
                    query_tile = grouped[q_first : q_first + tile_length]
                    kv_tile = source[k_first : k_first + tile_length]
                    scores = (
                        jnp.einsum(
                            "qhgd,khd->qhgk",
                            query_tile,
                            kv_tile[:, :, :HEAD_SIZE],
                            preferred_element_type=jnp.float32,
                        )
                        * inv_root
                    )
                    q_pos = query_start + q_first + offsets
                    k_pos = key_start + k_first + offsets
                    q_doc_t = query_doc_tiles[q_block]
                    q_span_t = query_span_tiles[q_block]
                    k_doc_t = key_doc_tiles[k_block]
                    k_span_t = key_span_tiles[k_block]
                    allowed = (
                        (q_doc_t[:, None] == k_doc_t[None, :])
                        & (q_span_t[:, None] == k_span_t[None, :])
                        & (k_pos[None, :] <= q_pos[:, None])
                    )
                    weights = jnp.where(allowed[:, None, None, :], jnp.exp(scores), 0.0)
                    part_den = jnp.sum(weights, axis=3)
                    part_num = jnp.einsum(
                        "qhgk,khd->qhgd",
                        weights.astype(jnp.bfloat16),
                        kv_tile[:, :, HEAD_SIZE:],
                        preferred_element_type=jnp.float32,
                    )
                    return (numer_in + part_num, denom_in + part_den)

                numer_list[q_block], denom_list[q_block] = lax.cond(
                    live_table[q_block, k_block],
                    compute,
                    lambda inner_acc: inner_acc,
                    (numer_list[q_block], denom_list[q_block]),
                )
    numerator = jnp.concatenate(numer_list, axis=0)
    denominator = jnp.concatenate(denom_list, axis=0)
    attended = (
        (numerator / denominator[..., None])
        .astype(jnp.bfloat16)
        .reshape(shard_len, local_heads, HEAD_SIZE)
    )
    returned = lax.all_to_all(attended, "exp", split_axis=0, concat_axis=1, tiled=True)
    return returned.reshape(shard_rows, QUERY_HEADS * HEAD_SIZE)


def unit_tile(tile):
    widened = tile.astype(jnp.float32)
    factor = lax.rsqrt(jnp.mean(widened * widened, axis=-1, keepdims=True) + 1e-06)
    return (widened * factor).astype(jnp.bfloat16)


def relay_kernel(
    blocks, lanes, q_ref, k_ref, v_ref, doc_ref, span_ref, out_ref,
    q_raw, q_unit, k_all, v_all, id_all, own_col, acc,
    own_sem, recv_sem, send_sem,
):
    rows = k_ref.shape[0]
    ctx = lax.axis_index("ctx")
    z = lax.axis_index("exp")
    even = ctx % 2 == 0
    slots = (k_all, v_all, id_all)
    inputs = (k_ref, v_ref, id_all.at[z])

    barrier = pltpu.get_barrier_semaphore()
    neighbours = [
        (z > 0, (ctx, z - 1)), (z < lanes - 1, (ctx, z + 1)),
        (ctx > 0, (ctx - 1, z)), (ctx < blocks - 1, (ctx + 1, z)),
        (ctx > 1, (ctx - 2, z)), (ctx < blocks - 2, (ctx + 2, z)),
    ]
    for present, device in neighbours:
        @pl.when(present)
        def _(device=device):
            pl.semaphore_signal(barrier, inc=1, device_id=device, device_id_type=MESH)
    pl.semaphore_wait(barrier, sum(present.astype(jnp.int32) for present, _ in neighbours))

    def send(way, b, zp, device, to_b, part, own, finish):
        copy = pltpu.make_async_remote_copy(
            src_ref=inputs[part] if own else slots[part].at[b * lanes + zp],
            dst_ref=slots[part].at[to_b * lanes + zp],
            send_sem=send_sem.at[way, b * lanes + zp, part],
            recv_sem=recv_sem.at[to_b * lanes + zp, part],
            device_id=device,
            device_id_type=MESH,
        )
        if finish:
            copy.wait_send()
        else:
            copy.start()

    def forward(b, zp, parts=(0, 1, 2), ways=(0, 1, 2, 3), also=True, own=False, finish=False):
        routes = []
        if b <= 1:
            routes.append((1, even & (z > 0) & (zp >= z), (ctx, z - 1), b))
        if b == 0:
            routes.append((2, even | ((zp <= z) & (ctx < blocks - 1)), (ctx + 1, z), 1))
            routes.append((0, (zp <= z) & (z < lanes - 1), (ctx, z + 1), 0))
            routes.append((3, even & (zp >= z) & (ctx < blocks - 2), (ctx + 2, z), 2))
        if b == 1:
            routes.append((2, even & (zp >= z), (ctx + 1, z), 2))
        for way, taken, device, to_b in routes:
            if way in ways:
                @pl.when(taken & also)
                def _(way=way, device=device, to_b=to_b):
                    for part in parts:
                        send(way, b, zp, device, to_b, part, own, finish)

    forward(0, z, parts=(0, 1), ways=(1, 2), own=True)
    forward(0, z, parts=(0, 1), ways=(0,), also=~even, own=True)

    id_copies = [
        pltpu.make_async_copy(ref, id_all.at[z, pl.ds(row, 1)], own_sem.at[row])
        for row, ref in enumerate((doc_ref, span_ref))
    ]
    own_copies = [
        pltpu.make_async_copy(inputs[part], slots[part].at[z], own_sem.at[2 + part]) for part in range(2)
    ]
    q_copy = pltpu.make_async_copy(q_ref, q_raw, own_sem.at[4])
    for copy in id_copies + [q_copy] + own_copies:
        copy.start()
    for copy in id_copies:
        copy.wait()
    forward(0, z, parts=(2,), ways=(1, 2), own=True)
    forward(0, z, parts=(2,), ways=(0,), also=~even, own=True)
    acc[...] = jnp.zeros_like(acc)
    q_copy.wait()

    @pl.loop(0, KEY_VALUE_HEADS, unroll=4)
    def _(g):
        for j in range(GROUP):
            column = pl.multiple_of((g * GROUP + j) * HEAD_SIZE, HEAD_SIZE)
            q_unit[g, pl.ds(j * rows, rows), :] = unit_tile(q_raw[:, pl.ds(column, HEAD_SIZE)])

    for copy in own_copies:
        copy.wait()

    def codes(slot):
        ids = id_all[slot]
        return jnp.broadcast_to(ids[0:1, :] * 65536 + ids[1:2, :], (rows, rows))

    own_col[...] = codes(z).T

    scale = math.log2(math.e) * HEAD_SIZE ** (-0.5)

    def attend(slot, own=False):
        same = own_col[...] == codes(slot)
        if own:
            same = same & (
                lax.broadcasted_iota(jnp.int32, (rows, rows), 1)
                <= lax.broadcasted_iota(jnp.int32, (rows, rows), 0)
            )
        kept = same.astype(jnp.float32).astype(jnp.bfloat16)
        ones = jnp.ones((rows, HEAD_SIZE), jnp.bfloat16)

        @pl.loop(0, KEY_VALUE_HEADS, unroll=KEY_VALUE_HEADS)
        def _(g):
            column = pl.ds(pl.multiple_of(g * HEAD_SIZE, HEAD_SIZE), HEAD_SIZE)
            key = unit_tile(k_all[slot, :, column])
            scores = lax.dot_general(
                q_unit[g], key, (((1,), (1,)), ((), ())), preferred_element_type=jnp.float32
            )
            weights = jnp.exp2(scores * scale).astype(jnp.bfloat16)
            weights = jnp.concatenate(
                [weights[j * rows : (j + 1) * rows] * kept for j in range(GROUP)], axis=0
            )
            value = jnp.concatenate([v_all[slot, :, column], ones], axis=1)
            acc[g] += jnp.dot(weights, value, preferred_element_type=jnp.float32)

    attend(z, own=True)
    forward(0, z, ways=(0,), also=even, own=True)
    forward(0, z, ways=(3,), own=True)

    def receive(b, zp, needed):
        slot = b * lanes + zp
        for part in range(3):
            pltpu.make_async_remote_copy(
                src_ref=slots[part].at[slot],
                dst_ref=slots[part].at[slot],
                send_sem=send_sem.at[0, slot, part],
                recv_sem=recv_sem.at[slot, part],
                device_id=(ctx, z),
                device_id_type=MESH,
            ).wait_recv()
            forward(b, zp, parts=(part,))
        if needed:
            attend(slot)

    late = (z > 0).astype(jnp.int32)

    @pl.loop(0, lanes + 1)
    def _(d):
        e = d - late
        for b, zp, valid, needed in (
            (0, z + d + 1, even & (z + d + 1 < lanes), False),
            (1, z + d, (ctx > 0) & (z + d < lanes), True),
            (0, z - d - 1, z - d - 1 >= 0, True),
            (1, z - e, (ctx > 0) & (z - e >= 0) & (e > 0), True),
            (2, z + e, (ctx > 1) & (z + e < lanes) & (e >= 0), True),
        ):
            @pl.when(valid)
            def _(b=b, zp=zp, needed=needed):
                receive(b, zp, needed)

    @pl.loop(0, KEY_VALUE_HEADS, unroll=4)
    def _(g):
        for j in range(GROUP):
            column = pl.multiple_of((g * GROUP + j) * HEAD_SIZE, HEAD_SIZE)
            part = acc[g, pl.ds(j * rows, rows), :]
            out_ref[:, pl.ds(column, HEAD_SIZE)] = (
                part[:, :HEAD_SIZE] / part[:, HEAD_SIZE:]
            ).astype(jnp.bfloat16)

    @pl.loop(0, lanes)
    def _(zp):
        @pl.when((zp <= z) | even)
        def _():
            forward(0, zp, finish=True)

        @pl.when(ctx > 0)
        def _():
            forward(1, zp, finish=True)


def relayed(queries, keys, values, doc_ids, span_ids):
    lanes = lax.axis_size("exp")
    blocks = lax.axis_size("ctx")
    rows = queries.shape[0]
    count = 3 * lanes
    bf16, f32 = jnp.bfloat16, jnp.float32
    return pl.pallas_call(
        lambda *refs: relay_kernel(blocks, lanes, *refs),
        out_shape=pltpu.VMEM(queries.shape, bf16),
        in_specs=[pl.BlockSpec(memory_space=pltpu.HBM)] * 5,
        out_specs=pl.BlockSpec(memory_space=pltpu.VMEM),
        scratch_shapes=[
            pltpu.VMEM(queries.shape, bf16),
            pltpu.VMEM((KEY_VALUE_HEADS, GROUP * rows, HEAD_SIZE), bf16),
            pltpu.VMEM((count,) + keys.shape, bf16),
            pltpu.VMEM((count,) + values.shape, bf16),
            pltpu.VMEM((count, 2, rows), jnp.int32),
            pltpu.VMEM((rows, rows), jnp.int32),
            pltpu.VMEM((KEY_VALUE_HEADS, GROUP * rows, 2 * HEAD_SIZE), f32),
            pltpu.SemaphoreType.DMA((5,)),
            pltpu.SemaphoreType.DMA((count, 3)),
            pltpu.SemaphoreType.DMA((4, count, 3)),
        ],
        compiler_params=pltpu.CompilerParams(collective_id=0, has_side_effects=True, vmem_limit_bytes=60 << 20),
    )(queries, keys, values, doc_ids[None, :], span_ids[None, :])


def per_device(queries, keys, values, doc_ids, span_ids):
    lanes, blocks = lax.axis_size("exp"), lax.axis_size("ctx")
    rows = queries.shape[0]
    tokens = rows * lanes * blocks
    reach = min(SPAN, DOC_LEN if tokens > PACKED_TOKENS else DOC_TOP)
    if reach <= 2 * lanes * rows and blocks % 2 == 0 and lanes <= 8 and rows % 128 == 0:
        return relayed(queries, keys, values, doc_ids, span_ids)
    return general(queries, keys, values, doc_ids, span_ids)


def solution(mesh):
    in_specs = (
        P(("ctx", "exp"), None),
        P(("ctx", "exp"), None),
        P(("ctx", "exp"), None),
        P(("ctx", "exp")),
        P(("ctx", "exp")),
    )
    out_specs = P(("ctx", "exp"), None)
    return jax.shard_map(
        per_device, mesh=mesh, in_specs=in_specs, out_specs=out_specs, check_vma=False
    )
```

```python
import math

import jax
import jax.numpy as jnp
from jax import lax
from jax.experimental import pallas as pl
from jax.experimental.pallas import tpu as pltpu
from jax.sharding import PartitionSpec as P

QUERY_HEADS = 32
KEY_VALUE_HEADS = 8
HEAD_SIZE = 128
SPAN = 8192
DOC_LEN = 2048
PACKED_TOKENS = 4096
DOC_TOP = 1024
GROUP = QUERY_HEADS // KEY_VALUE_HEADS
MESH = pl.DeviceIdType.MESH


def shifted(block, axis, distance):
    devices = range(lax.axis_size(axis))
    route = [(i - distance, i) for i in devices if i - distance in devices]
    return lax.ppermute(block, axis, route)


def single_unit_rows(tensor):
    widened = tensor.astype(jnp.float32)
    factor = lax.rsqrt(jnp.mean(widened * widened, axis=-1, keepdims=True) + 1e-06)
    return (widened * factor).astype(jnp.bfloat16)


def general(queries, keys, values, doc_ids, span_ids):
    expanded_size = lax.axis_size("exp")
    ctx_size = lax.axis_size("ctx")
    shard_rows = queries.shape[0]
    shard_len = shard_rows * expanded_size
    query_heads = single_unit_rows(queries.reshape(shard_rows, QUERY_HEADS, HEAD_SIZE))
    key_head_rows = single_unit_rows(keys.reshape(shard_rows, KEY_VALUE_HEADS, HEAD_SIZE))
    value_head_rows = values.reshape(shard_rows, KEY_VALUE_HEADS, HEAD_SIZE)
    head_replicas = max(1, expanded_size // KEY_VALUE_HEADS)
    reach_len = min(SPAN, DOC_LEN)
    steps_back = min((reach_len - 2) // shard_len + 1, ctx_size - 1)
    raw_pair = jnp.concatenate([key_head_rows, value_head_rows], axis=2)

    def spread(pair_rows):
        if head_replicas > 1:
            return jnp.repeat(pair_rows, head_replicas, axis=1)
        return pair_rows

    sources = []
    paired = spread(raw_pair)
    query_local, pair_local = (
        lax.all_to_all(query_heads, "exp", split_axis=1, concat_axis=0, tiled=True),
        lax.all_to_all(paired, "exp", split_axis=1, concat_axis=0, tiled=True),
    )
    block_doc, block_span = (
        lax.all_gather(doc_ids, "exp", axis=0, tiled=True),
        lax.all_gather(span_ids, "exp", axis=0, tiled=True),
    )
    sources.append((0, pair_local, block_doc, block_span))
    for distance in range(1, steps_back + 1):
        moved = shifted(pair_local, "ctx", distance)
        moved_doc, moved_span = shifted((block_doc, block_span), "ctx", distance)
        sources.append((distance, moved, moved_doc, moved_span))
    block_doc = sources[0][2]
    block_span = sources[0][3]
    local_heads = query_local.shape[1]
    pair_heads = sources[0][1].shape[1]
    query_group_width = local_heads // pair_heads
    ctx_index = lax.axis_index("ctx")
    tile_length = min(512, shard_len)
    tiles_side = shard_len // tile_length
    query_start = ctx_index * shard_len
    grouped = query_local.reshape(shard_len, pair_heads, query_group_width, HEAD_SIZE)
    inv_root = HEAD_SIZE ** (-0.5)
    offsets = jnp.arange(tile_length, dtype=jnp.int32)
    query_doc_tiles = block_doc.reshape(tiles_side, tile_length)
    query_span_tiles = block_span.reshape(tiles_side, tile_length)
    numer_list = [
        jnp.zeros((tile_length, pair_heads, query_group_width, HEAD_SIZE), jnp.float32)
        for _ in range(tiles_side)
    ]
    denom_list = [
        jnp.zeros((tile_length, pair_heads, query_group_width), jnp.float32)
        for _ in range(tiles_side)
    ]
    for distance, source, key_doc, key_span in sources:
        key_start = query_start - distance * shard_len
        present = ctx_index >= distance
        key_doc_tiles = key_doc.reshape(tiles_side, tile_length)
        key_span_tiles = key_span.reshape(tiles_side, tile_length)
        live_table = (
            (key_doc_tiles[None, :, tile_length - 1] >= query_doc_tiles[:, None, 0])
            & (key_span_tiles[None, :, tile_length - 1] >= query_span_tiles[:, None, 0])
            & present
        )
        for q_block in range(tiles_side):
            for k_block in range(tiles_side):
                q_first = q_block * tile_length
                k_first = k_block * tile_length
                static_gap = distance * shard_len + q_first - k_first
                if static_gap + tile_length - 1 < 0:
                    continue
                if static_gap - (tile_length - 1) > reach_len - 1:
                    continue

                def compute(
                    inner_acc,
                    source=source,
                    key_start=key_start,
                    q_first=q_first,
                    k_first=k_first,
                    key_doc_tiles=key_doc_tiles,
                    key_span_tiles=key_span_tiles,
                    q_block=q_block,
                    k_block=k_block,
                ):
                    numer_in, denom_in = inner_acc
                    query_tile = grouped[q_first : q_first + tile_length]
                    kv_tile = source[k_first : k_first + tile_length]
                    scores = (
                        jnp.einsum(
                            "qhgd,khd->qhgk",
                            query_tile,
                            kv_tile[:, :, :HEAD_SIZE],
                            preferred_element_type=jnp.float32,
                        )
                        * inv_root
                    )
                    q_pos = query_start + q_first + offsets
                    k_pos = key_start + k_first + offsets
                    q_doc_t = query_doc_tiles[q_block]
                    q_span_t = query_span_tiles[q_block]
                    k_doc_t = key_doc_tiles[k_block]
                    k_span_t = key_span_tiles[k_block]
                    allowed = (
                        (q_doc_t[:, None] == k_doc_t[None, :])
                        & (q_span_t[:, None] == k_span_t[None, :])
                        & (k_pos[None, :] <= q_pos[:, None])
                    )
                    weights = jnp.where(allowed[:, None, None, :], jnp.exp(scores), 0.0)
                    part_den = jnp.sum(weights, axis=3)
                    part_num = jnp.einsum(
                        "qhgk,khd->qhgd",
                        weights.astype(jnp.bfloat16),
                        kv_tile[:, :, HEAD_SIZE:],
                        preferred_element_type=jnp.float32,
                    )
                    return (numer_in + part_num, denom_in + part_den)

                numer_list[q_block], denom_list[q_block] = lax.cond(
                    live_table[q_block, k_block],
                    compute,
                    lambda inner_acc: inner_acc,
                    (numer_list[q_block], denom_list[q_block]),
                )
    numerator = jnp.concatenate(numer_list, axis=0)
    denominator = jnp.concatenate(denom_list, axis=0)
    attended = (
        (numerator / denominator[..., None])
        .astype(jnp.bfloat16)
        .reshape(shard_len, local_heads, HEAD_SIZE)
    )
    returned = lax.all_to_all(attended, "exp", split_axis=0, concat_axis=1, tiled=True)
    return returned.reshape(shard_rows, QUERY_HEADS * HEAD_SIZE)


def unit_tile(tile):
    widened = tile.astype(jnp.float32)
    factor = lax.rsqrt(jnp.mean(widened * widened, axis=-1, keepdims=True) + 1e-06)
    return (widened * factor).astype(jnp.bfloat16)


def relay_kernel(
    blocks, lanes, q_ref, k_ref, v_ref, doc_ref, span_ref, out_ref,
    q_raw, q_unit, k_all, v_all, id_all, own_col, acc,
    own_sem, recv_sem, send_sem,
):
    rows = k_ref.shape[0]
    ctx = lax.axis_index("ctx")
    z = lax.axis_index("exp")
    even = ctx % 2 == 0
    slots = (k_all, v_all, id_all)
    inputs = (k_ref, v_ref, id_all.at[z])

    barrier = pltpu.get_barrier_semaphore()
    neighbours = [
        (z > 0, (ctx, z - 1)), (z < lanes - 1, (ctx, z + 1)),
        (ctx > 0, (ctx - 1, z)), (ctx < blocks - 1, (ctx + 1, z)),
        (ctx > 1, (ctx - 2, z)), (ctx < blocks - 2, (ctx + 2, z)),
    ]
    for present, device in neighbours:
        @pl.when(present)
        def _(device=device):
            pl.semaphore_signal(barrier, inc=1, device_id=device, device_id_type=MESH)
    pl.semaphore_wait(barrier, sum(present.astype(jnp.int32) for present, _ in neighbours))

    def send(way, b, zp, device, to_b, part, own, finish):
        copy = pltpu.make_async_remote_copy(
            src_ref=inputs[part] if own else slots[part].at[b * lanes + zp],
            dst_ref=slots[part].at[to_b * lanes + zp],
            send_sem=send_sem.at[way, b * lanes + zp, part],
            recv_sem=recv_sem.at[to_b * lanes + zp, part],
            device_id=device,
            device_id_type=MESH,
        )
        if finish:
            copy.wait_send()
        else:
            copy.start()

    def forward(b, zp, parts=(0, 1, 2), ways=(0, 1, 2, 3), also=True, own=False, finish=False):
        routes = []
        if b <= 1:
            routes.append((1, even & (z > 0) & (zp >= z), (ctx, z - 1), b))
        if b == 0:
            routes.append((2, even | ((zp <= z) & (ctx < blocks - 1)), (ctx + 1, z), 1))
            routes.append((0, (zp <= z) & (z < lanes - 1), (ctx, z + 1), 0))
            routes.append((3, even & (zp >= z) & (ctx < blocks - 2), (ctx + 2, z), 2))
        if b == 1:
            routes.append((2, even & (zp >= z), (ctx + 1, z), 2))
        for way, taken, device, to_b in routes:
            if way in ways:
                @pl.when(taken & also)
                def _(way=way, device=device, to_b=to_b):
                    for part in parts:
                        send(way, b, zp, device, to_b, part, own, finish)

    forward(0, z, parts=(0, 1), ways=(1, 2), own=True)
    forward(0, z, parts=(0, 1), ways=(0,), also=~even, own=True)

    id_copies = [
        pltpu.make_async_copy(ref, id_all.at[z, pl.ds(row, 1)], own_sem.at[row])
        for row, ref in enumerate((doc_ref, span_ref))
    ]
    own_copies = [
        pltpu.make_async_copy(inputs[part], slots[part].at[z], own_sem.at[2 + part]) for part in range(2)
    ]
    q_copy = pltpu.make_async_copy(q_ref, q_raw, own_sem.at[4])
    for copy in id_copies + [q_copy] + own_copies:
        copy.start()
    for copy in id_copies:
        copy.wait()
    forward(0, z, parts=(2,), ways=(1, 2), own=True)
    forward(0, z, parts=(2,), ways=(0,), also=~even, own=True)
    acc[...] = jnp.zeros_like(acc)
    q_copy.wait()

    @pl.loop(0, KEY_VALUE_HEADS, unroll=4)
    def _(g):
        for j in range(GROUP):
            column = pl.multiple_of((g * GROUP + j) * HEAD_SIZE, HEAD_SIZE)
            q_unit[g, pl.ds(j * rows, rows), :] = unit_tile(q_raw[:, pl.ds(column, HEAD_SIZE)])

    for copy in own_copies:
        copy.wait()

    def codes(slot):
        ids = id_all[slot]
        return jnp.broadcast_to(ids[0:1, :] * 65536 + ids[1:2, :], (rows, rows))

    own_col[...] = codes(z).T

    scale = math.log2(math.e) * HEAD_SIZE ** (-0.5)

    def attend(slot, own=False):
        same = own_col[...] == codes(slot)
        if own:
            same = same & (
                lax.broadcasted_iota(jnp.int32, (rows, rows), 1)
                <= lax.broadcasted_iota(jnp.int32, (rows, rows), 0)
            )
        kept = same.astype(jnp.float32).astype(jnp.bfloat16)
        ones = jnp.ones((rows, HEAD_SIZE), jnp.bfloat16)

        @pl.loop(0, KEY_VALUE_HEADS, unroll=KEY_VALUE_HEADS)
        def _(g):
            column = pl.ds(pl.multiple_of(g * HEAD_SIZE, HEAD_SIZE), HEAD_SIZE)
            key = unit_tile(k_all[slot, :, column])
            scores = lax.dot_general(
                q_unit[g], key, (((1,), (1,)), ((), ())), preferred_element_type=jnp.float32
            )
            weights = jnp.exp2(scores * scale).astype(jnp.bfloat16)
            weights = jnp.concatenate(
                [weights[j * rows : (j + 1) * rows] * kept for j in range(GROUP)], axis=0
            )
            value = jnp.concatenate([v_all[slot, :, column], ones], axis=1)
            acc[g] += jnp.dot(weights, value, preferred_element_type=jnp.float32)

    attend(z, own=True)
    forward(0, z, ways=(0,), also=even, own=True)
    forward(0, z, ways=(3,), own=True)

    def receive(b, zp, needed):
        slot = b * lanes + zp
        for part in range(3):
            pltpu.make_async_remote_copy(
                src_ref=slots[part].at[slot],
                dst_ref=slots[part].at[slot],
                send_sem=send_sem.at[0, slot, part],
                recv_sem=recv_sem.at[slot, part],
                device_id=(ctx, z),
                device_id_type=MESH,
            ).wait_recv()
            forward(b, zp, parts=(part,))
        if needed:
            attend(slot)

    late = 2 * ((z > 0) & (z < lanes - 1)).astype(jnp.int32)

    @pl.loop(0, lanes + 2)
    def _(d):
        e = d - late
        for b, zp, valid, needed in (
            (1, z - e, (ctx > 0) & (z - e >= 0) & (e > 0), True),
            (2, z + e, (ctx > 1) & (z + e < lanes) & (e >= 0), True),
            (0, z + d + 1, even & (z + d + 1 < lanes), False),
            (1, z + d, (ctx > 0) & (z + d < lanes), True),
            (0, z - d - 1, z - d - 1 >= 0, True),
        ):
            @pl.when(valid)
            def _(b=b, zp=zp, needed=needed):
                receive(b, zp, needed)

    @pl.loop(0, KEY_VALUE_HEADS, unroll=4)
    def _(g):
        for j in range(GROUP):
            column = pl.multiple_of((g * GROUP + j) * HEAD_SIZE, HEAD_SIZE)
            part = acc[g, pl.ds(j * rows, rows), :]
            out_ref[:, pl.ds(column, HEAD_SIZE)] = (
                part[:, :HEAD_SIZE] / part[:, HEAD_SIZE:]
            ).astype(jnp.bfloat16)

    @pl.loop(0, lanes)
    def _(zp):
        @pl.when((zp <= z) | even)
        def _():
            forward(0, zp, finish=True)

        @pl.when(ctx > 0)
        def _():
            forward(1, zp, finish=True)


def relayed(queries, keys, values, doc_ids, span_ids):
    lanes = lax.axis_size("exp")
    blocks = lax.axis_size("ctx")
    rows = queries.shape[0]
    count = 3 * lanes
    bf16, f32 = jnp.bfloat16, jnp.float32
    return pl.pallas_call(
        lambda *refs: relay_kernel(blocks, lanes, *refs),
        out_shape=pltpu.VMEM(queries.shape, bf16),
        in_specs=[pl.BlockSpec(memory_space=pltpu.HBM)] * 5,
        out_specs=pl.BlockSpec(memory_space=pltpu.VMEM),
        scratch_shapes=[
            pltpu.VMEM(queries.shape, bf16),
            pltpu.VMEM((KEY_VALUE_HEADS, GROUP * rows, HEAD_SIZE), bf16),
            pltpu.VMEM((count,) + keys.shape, bf16),
            pltpu.VMEM((count,) + values.shape, bf16),
            pltpu.VMEM((count, 2, rows), jnp.int32),
            pltpu.VMEM((rows, rows), jnp.int32),
            pltpu.VMEM((KEY_VALUE_HEADS, GROUP * rows, 2 * HEAD_SIZE), f32),
            pltpu.SemaphoreType.DMA((5,)),
            pltpu.SemaphoreType.DMA((count, 3)),
            pltpu.SemaphoreType.DMA((4, count, 3)),
        ],
        compiler_params=pltpu.CompilerParams(collective_id=0, has_side_effects=True, vmem_limit_bytes=60 << 20),
    )(queries, keys, values, doc_ids[None, :], span_ids[None, :])


def per_device(queries, keys, values, doc_ids, span_ids):
    lanes, blocks = lax.axis_size("exp"), lax.axis_size("ctx")
    rows = queries.shape[0]
    tokens = rows * lanes * blocks
    reach = min(SPAN, DOC_LEN if tokens > PACKED_TOKENS else DOC_TOP)
    if reach <= 2 * lanes * rows and blocks % 2 == 0 and lanes <= 8 and rows % 128 == 0:
        return relayed(queries, keys, values, doc_ids, span_ids)
    return general(queries, keys, values, doc_ids, span_ids)


def solution(mesh):
    in_specs = (
        P(("ctx", "exp"), None),
        P(("ctx", "exp"), None),
        P(("ctx", "exp"), None),
        P(("ctx", "exp")),
        P(("ctx", "exp")),
    )
    out_specs = P(("ctx", "exp"), None)
    return jax.shard_map(
        per_device, mesh=mesh, in_specs=in_specs, out_specs=out_specs, check_vma=False
    )
```
